256 devices in a mesh: ctx: 64 (over z, y, x_lo), tp: 4 (over x_hi, core).
Axes of the slice: x: 4 (x_hi: 2, x_lo: 2; x = x_hi * 2 + x_lo), y: 4, z: 8, core: 2. Of those that a mesh axis runs over, the one named last changes fastest.
Arguments:
- key_act: bfloat16 [16384, 2048], P('ctx', 'tp'), may hold values from -6 to 6
- value_act: bfloat16 [16384, 2048], P('ctx', 'tp'), may hold values from -6 to 6
- query_act: bfloat16 [16384, 2048], P('ctx', 'tp'), may hold values from -6 to 6
- grad_out: bfloat16 [16384, 2048], P('ctx', 'tp'), may hold values from -6 to 6
- long_filter: bfloat16 [16384, 2048], P('ctx', 'tp'), may hold values from -6 to 6
- w_key: bfloat16 [2048, 2048], P(None, 'tp'), may hold values from -0.125 to 0.125
- w_query: bfloat16 [2048, 2048], P(None, 'tp'), may hold values from -0.125 to 0.125
- w_value: bfloat16 [2048, 2048], P(None, 'tp'), may hold values from -0.125 to 0.125
Outputs:
- grad_input: bfloat16 [16384, 2048], P('ctx', 'tp')
- grad_filter: bfloat16 [16384, 2048], P('ctx', 'tp')
The draws below stay inside these ranges and needn't reach their ends.
All inputs are finite; a program needn't handle non-finite values.
Results may differ from the reference program's by a relative error of at most 0.025.
Values may be sent and summed in bfloat16 or wider, within the bound.
A program may use at most 128 MiB of HBM per device.

```python
import math
import jax
import jax.numpy as jnp
from jax import lax

D = 2048
SEQ = 16384
N_TP = 4


def shard_levels(own_key, shape, cuts, low, top_value):
    level, own = 1.0, jax.random.fold_in(own_key, 6)
    for position, blocks in cuts:
        draws = jnp.exp(jax.random.uniform(jax.random.fold_in(own, position), (blocks,), jnp.float32, low / len(cuts), top_value / len(cuts)))
        level = level * jnp.repeat(draws, shape[position] // blocks).reshape([-1 if axis == position else 1 for axis in range(len(shape))])
    return level


def gaussian(own_key, dims, scale, bound, split=(), dtype=jnp.bfloat16):
    level = shard_levels(own_key, dims, split, -0.22, 0.18) if split else 1.0
    array = jax.random.normal(own_key, dims, jnp.float32) * scale * level
    return jnp.minimum(jnp.maximum(array, -bound), bound).astype(dtype)


def setup_inputs(seed: int = 0) -> dict:
    keys = jax.random.split(jax.random.key(seed), 9)
    key_act = gaussian(keys[0], (SEQ, D), 1.0, 6.0, ((0, 64), (1, 4)))
    value_act = gaussian(keys[1], (SEQ, D), 1.0, 6.0, ((0, 64), (1, 4)))
    query_act = gaussian(keys[2], (SEQ, D), 1.0, 6.0, ((0, 64), (1, 4)))
    grad_out = gaussian(keys[3], (SEQ, D), 1.0, 6.0, ((0, 64), (1, 4)))
    long_filter = gaussian(keys[4], (SEQ, D), 1.0, 6.0, ((0, 64), (1, 4)))
    w_key = gaussian(keys[5], (D, D), D ** -0.5, 0.125, ((1, 4),))
    w_query = gaussian(keys[6], (D, D), D ** -0.5, 0.125, ((1, 4),))
    w_value = gaussian(keys[7], (D, D), D ** -0.5, 0.125, ((1, 4),))
    return {"key_act": key_act, "value_act": value_act, "query_act": query_act, "grad_out": grad_out, "long_filter": long_filter, "w_key": w_key, "w_query": w_query, "w_value": w_value}


def convolve_block(stacked):
    product = stacked[0]
    kernel_raw = stacked[1]
    gated = stacked[2]
    padded_len = 2 * SEQ
    factor = 1.0 / math.sqrt(SEQ)
    spec_prod = jnp.fft.rfft(product, n=padded_len, axis=0)
    spec_kern = jnp.fft.rfft(kernel_raw, n=padded_len, axis=0) * factor
    spec_grad = jnp.fft.rfft(gated, n=padded_len, axis=0)
    conv_out = jnp.fft.irfft(spec_prod * spec_kern, n=padded_len, axis=0)[:SEQ]
    grad_product = jnp.fft.irfft(spec_grad * jnp.conj(spec_kern), n=padded_len, axis=0)[:SEQ]
    grad_filter = jnp.fft.irfft(spec_grad * jnp.conj(spec_prod), n=padded_len, axis=0)[:SEQ] * factor
    return jnp.stack([conv_out, grad_product, grad_filter]).astype(jnp.float32).astype(jnp.bfloat16)

def reference(key_act, value_act, query_act, grad_out, long_filter, w_key, w_query, w_value):
    product = (key_act.astype(jnp.float32) * value_act.astype(jnp.float32)).astype(jnp.bfloat16)
    gated = (grad_out.astype(jnp.float32) * query_act.astype(jnp.float32)).astype(jnp.bfloat16)
    width = 128 if D % 128 == 0 else D
    count = D // width
    stacked = jnp.stack([product.astype(jnp.float32), long_filter.astype(jnp.float32), gated.astype(jnp.float32)])
    blocked = stacked.reshape(3, SEQ, count, width).transpose(2, 0, 1, 3)
    outputs = lax.map(convolve_block, blocked)
    outputs = outputs.transpose(1, 2, 0, 3).reshape(3, SEQ, D)
    conv_out = outputs[0].astype(jnp.float32)
    grad_product = outputs[1].astype(jnp.float32)
    grad_filter = outputs[2]
    grad_key = (grad_product * value_act.astype(jnp.float32)).astype(jnp.bfloat16)
    grad_query = (conv_out * grad_out.astype(jnp.float32)).astype(jnp.bfloat16)
    grad_value = (grad_product * key_act.astype(jnp.float32)).astype(jnp.bfloat16)
    contract_dims = (((1,), (1,)), ((), ()))
    group_width = D // N_TP
    accumulated = jnp.zeros((SEQ, D), jnp.float32)
    for group_index in range(N_TP):
        start_col = group_index * group_width
        stop_col = start_col + group_width
        group_term = lax.dot_general(grad_key[:, start_col:stop_col], w_key[:, start_col:stop_col], contract_dims, preferred_element_type=jnp.float32)
        group_term = group_term + lax.dot_general(grad_query[:, start_col:stop_col], w_query[:, start_col:stop_col], contract_dims, preferred_element_type=jnp.float32)
        group_term = group_term + lax.dot_general(grad_value[:, start_col:stop_col], w_value[:, start_col:stop_col], contract_dims, preferred_element_type=jnp.float32)
        rounded = lax.optimization_barrier(group_term.astype(jnp.bfloat16))
        accumulated = accumulated + rounded.astype(jnp.float32)
    return (accumulated.astype(jnp.bfloat16), grad_filter)
```

```python
import functools
import math

import jax
import jax.numpy as jnp
import numpy as np
from jax import lax
from jax.experimental import pallas as pl
from jax.experimental.pallas import tpu as pltpu
from jax.sharding import PartitionSpec as P

f32 = jnp.float32
bf16 = jnp.bfloat16
BLOCKS = 64
CH = 8
LEN = 256
ROWS = BLOCKS * CH
WIDTH = 512
D_OUT = 2048
HALF = 256


def tables():
    total = BLOCKS * LEN
    k = np.arange(BLOCKS)
    b = np.arange(LEN)
    first = np.exp(-2j * np.pi * np.outer(k + 0.25, k) / BLOCKS)
    twist = np.exp(-2j * np.pi * np.outer(k + 0.25, b) / total)
    second = np.exp(-2j * np.pi * np.outer(b, b) / LEN)
    eye = np.eye(CH)
    fwd1 = np.kron(np.concatenate([first.real, first.imag]), eye)
    scale = 1.0 / (total * math.sqrt(total))
    inv1 = np.kron(np.concatenate([first.real.T, first.imag.T], 1), eye) * scale
    fwd2 = np.block([[second.real, second.imag], [-second.imag, second.real]])
    inv2 = np.block([[second.real, -second.imag], [second.imag, second.real]])
    cast = lambda a, t: jnp.asarray(np.asarray(a, np.float32)).astype(t)
    rep = lambda a: np.repeat(a, CH, 0)
    return (
        cast(fwd1, bf16),
        cast(fwd2, bf16),
        cast(inv2, bf16),
        cast(inv1, bf16),
        cast(rep(twist.real), f32),
        cast(rep(twist.imag), f32),
        cast(np.eye(HALF), bf16),
    )


def dot(a, b):
    return jnp.dot(a, b, preferred_element_type=f32)


def dot_nt(a, b):
    return lax.dot_general(a, b, (((1,), (1,)), ((), ())), preferred_element_type=f32)


def partner(me, i):
    z, y, x = me // 8, (me // 2) % 4, me % 2
    dz, r = i % 8, i // 8
    return ((z + dz) % 8) * 8 + ((y + r // 2) % 4) * 2 + (x + r % 2) % 2


def kernel(
    key_h, val_h, qry_h, gout_h, filt_h, wk_h, wq_h, wv_h,
    fwd1_h, fwd2_h, inv2_h, inv1_h, twr_h, twi_h, eye_h,
    gin_ref, gfil_ref,
    key, val, qry, gout, filt, wk, wq, wv,
    fwd1, fwd2, inv2, inv1, twr, twi, eye,
    key_t, val_t, gout_t,
    send, recv, xbuf, spec, ubuf, gbuf, acc,
    sib_out, sib_in, far_out, far_in, fin,
    in_sem, send_sem, recv_sem, rs_send, rs_recv,
):
    me = lax.axis_index("ctx")
    tp = lax.axis_index("tp")
    core = tp % 2
    sib = tp + 1 - 2 * core
    far = (tp + 2) % 4
    diag = 3 - tp

    pairs = [
        (filt_h, filt), (eye_h, eye), (qry_h, qry), (gout_h, gout), (key_h, key), (val_h, val),
        (fwd1_h, fwd1), (twr_h, twr), (twi_h, twi), (fwd2_h, fwd2), (inv2_h, inv2), (inv1_h, inv1),
        (wk_h, wk), (wv_h, wv), (wq_h, wq),
    ]
    loads = [pltpu.make_async_copy(s, d, in_sem.at[n]) for n, (s, d) in enumerate(pairs)]
    for load in loads:
        load.start()

    barrier = pltpu.get_barrier_semaphore()
    for t in (sib, far):
        pl.semaphore_signal(barrier, inc=1, device_id={"tp": t})

    @pl.loop(1, BLOCKS)
    def _(i):
        pl.semaphore_signal(barrier, inc=1, device_id={"ctx": partner(me, i)})

    def flip(src, h):
        return dot_nt(eye[...], src[:, pl.ds(h * HALF, HALF)])

    def post(n):
        pltpu.make_async_copy(send.at[n, me], recv.at[n, me], recv_sem.at[n]).start()

        @pl.loop(1, BLOCKS)
        def _(i):
            d = partner(me, i)
            pltpu.make_async_remote_copy(
                send.at[n, d], recv.at[n, me], send_sem.at[n], recv_sem.at[n],
                device_id={"ctx": d},
            ).start()

    def arrived(n):
        pltpu.make_async_copy(recv.at[n], recv.at[n], recv_sem.at[n]).wait()

    def put_send(n, h, values):
        send[n, pl.ds(h * 32, 32)] = values.reshape(32, CH, LEN).astype(bf16)

    def get_recv(n):
        return recv[n].astype(f32).reshape(ROWS, LEN)

    loads[0].wait()
    loads[1].wait()
    for h in range(2):
        put_send(0, h, flip(filt, h))
    pl.semaphore_wait(barrier, BLOCKS + 1)
    post(0)

    loads[2].wait()
    loads[3].wait()
    for h in range(2):
        rows = pl.ds(h * HALF, HALF)
        g = flip(gout, h)
        gout_t[rows, :] = g.astype(bf16)
        put_send(1, h, flip(qry, h) * g)
    post(1)

    loads[4].wait()
    loads[5].wait()
    for h in range(2):
        rows = pl.ds(h * HALF, HALF)
        a = flip(key, h)
        b = flip(val, h)
        key_t[rows, :] = a.astype(bf16)
        val_t[rows, :] = b.astype(bf16)
        put_send(2, h, a * b)
    post(2)

    def forward(n):
        xbuf[...] = get_recv(n).astype(bf16)

        @pl.loop(0, 2)
        def _(i):
            m = pl.multiple_of(i * HALF, HALF)
            rows = pl.ds(m, HALF)
            yr = dot(fwd1[rows, :], xbuf[...])
            yi = dot(fwd1[pl.ds(m + ROWS, HALF), :], xbuf[...])
            c, s = twr[rows, :], twi[rows, :]
            t = jnp.concatenate([yr * c - yi * s, yr * s + yi * c], axis=1).astype(bf16)
            spec[n, rows, :] = dot(t, fwd2[...])

    def inverse(na, nb, conj, out):
        @pl.loop(0, 2)
        def _(i):
            m = pl.multiple_of(i * HALF, HALF)
            rows = pl.ds(m, HALF)
            ar, ai = spec[na, rows, :LEN], spec[na, rows, LEN:]
            br, bi = spec[nb, rows, :LEN], spec[nb, rows, LEN:]
            if conj:
                yr, yi = ar * br + ai * bi, ai * br - ar * bi
            else:
                yr, yi = ar * br - ai * bi, ar * bi + ai * br
            t = dot(jnp.concatenate([yr, yi], axis=1).astype(bf16), inv2[...])
            tr, ti = t[:, :LEN], t[:, LEN:]
            c, s = twr[rows, :], twi[rows, :]
            ubuf[rows, :] = (tr * c + ti * s).astype(bf16)
            ubuf[pl.ds(m + ROWS, HALF), :] = (ti * c - tr * s).astype(bf16)

        @pl.loop(0, 2)
        def _(i):
            m = pl.multiple_of(i * HALF, HALF)
            y = dot(inv1[pl.ds(m, HALF), :], ubuf[...])
            send[out, pl.ds(i * 32, 32)] = y.reshape(32, CH, LEN).astype(bf16)

    for load in loads[6:12]:
        load.wait()
    arrived(0)
    forward(0)
    arrived(1)
    forward(1)
    inverse(1, 0, True, 3)
    post(3)
    arrived(2)
    forward(2)
    inverse(2, 0, False, 4)
    post(4)
    inverse(1, 2, True, 5)
    post(5)

    for load in loads[12:]:
        load.wait()
    arrived(3)
    back = get_recv(3)
    gbuf[0] = (back * val_t[...].astype(f32)).astype(bf16)
    gbuf[1] = (back * key_t[...].astype(f32)).astype(bf16)

    @pl.loop(0, D_OUT // HALF)
    def _(i):
        rows = pl.ds(pl.multiple_of(i * HALF, HALF), HALF)
        acc[rows, :] = dot(wk[rows, :], gbuf[0]) + dot(wv[rows, :], gbuf[1])

    arrived(4)
    gbuf[2] = (get_recv(4) * gout_t[...].astype(f32)).astype(bf16)

    def term(t):
        rows = pl.ds(pl.multiple_of(t * WIDTH, WIDTH), WIDTH)
        return acc[rows, :] + dot(wq[rows, :], gbuf[2])

    def to_sib(n):
        return pltpu.make_async_remote_copy(
            sib_out.at[n], sib_in.at[n], rs_send.at[n], rs_recv.at[n], device_id={"tp": sib}
        )

    to_far = pltpu.make_async_remote_copy(
        far_out, far_in, rs_send.at[2], rs_recv.at[2], device_id={"tp": far}
    )
    sib_out[0] = term(diag).astype(bf16)
    to_sib(0).start()
    mine = term(far)
    to_sib(0).wait_recv()
    far_out[...] = (mine + sib_in[0].astype(f32)).astype(bf16)
    to_far.start()
    sib_out[1] = term(sib).astype(bf16)
    to_sib(1).start()
    own = term(tp)
    to_sib(1).wait_recv()
    acc[pl.ds(0, WIDTH), :] = own + sib_in[1].astype(f32)

    arrived(5)
    gfil_ref[...] = dot_nt(eye[...], get_recv(5).astype(bf16)).astype(bf16)
    to_far.wait_recv()
    fin[...] = (acc[pl.ds(0, WIDTH), :] + far_in[...].astype(f32)).astype(bf16)
    gin_ref[...] = dot_nt(eye[...], fin[...]).astype(bf16)

    for n in range(6):
        some = send.at[n, pl.ds(0, BLOCKS - 1)]
        pltpu.make_async_copy(some, some, send_sem.at[n]).wait()
    to_sib(0).wait_send()
    to_sib(1).wait_send()
    to_far.wait_send()


def per_device(key_act, value_act, query_act, grad_out, long_filter, w_key, w_query, w_value):
    consts = tables()
    act = lambda: pltpu.VMEM((LEN, WIDTH), bf16)
    weight = lambda: pltpu.VMEM((D_OUT, WIDTH), bf16)
    turned = lambda: pltpu.VMEM((WIDTH, LEN), bf16)
    dma = pltpu.SemaphoreType.DMA
    return pl.pallas_call(
        kernel,
        out_shape=(jax.ShapeDtypeStruct((LEN, WIDTH), bf16),) * 2,
        in_specs=[pl.BlockSpec(memory_space=pl.ANY)] * 15,
        out_specs=[pl.BlockSpec(memory_space=pltpu.VMEM)] * 2,
        scratch_shapes=[act()] * 5
        + [weight()] * 3
        + [pltpu.VMEM(c.shape, c.dtype) for c in consts]
        + [turned()] * 3
        + [
            pltpu.VMEM((6, BLOCKS, CH, LEN), bf16),
            pltpu.VMEM((6, BLOCKS, CH, LEN), bf16),
            pltpu.VMEM((ROWS, LEN), bf16),
            pltpu.VMEM((3, ROWS, 2 * LEN), f32),
            pltpu.VMEM((2 * ROWS, LEN), bf16),
            pltpu.VMEM((3, WIDTH, LEN), bf16),
            pltpu.VMEM((D_OUT, LEN), f32),
            pltpu.VMEM((2, WIDTH, LEN), bf16),
            pltpu.VMEM((2, WIDTH, LEN), bf16),
            turned(),
            turned(),
            turned(),
            dma((15,)),
            dma((6,)),
            dma((6,)),
            dma((3,)),
            dma((3,)),
        ],
        compiler_params=pltpu.CompilerParams(
            collective_id=1, has_side_effects=True, vmem_limit_bytes=56 * 2**20
        ),
    )(key_act, value_act, query_act, grad_out, long_filter, w_key, w_query, w_value, *consts)


def solution(mesh):
    placed = (P("ctx", "tp"),) * 5 + (P(None, "tp"),) * 3
    return jax.shard_map(
        per_device,
        mesh=mesh,
        in_specs=placed,
        out_specs=(P("ctx", "tp"), P("ctx", "tp")),
        check_vma=False,
    )
```

```python
import functools
import math

import jax
import jax.numpy as jnp
import numpy as np
from jax import lax
from jax.experimental import pallas as pl
from jax.experimental.pallas import tpu as pltpu
from jax.sharding import PartitionSpec as P

f32 = jnp.float32
bf16 = jnp.bfloat16
BLOCKS = 64
CH = 8
LEN = 256
ROWS = BLOCKS * CH
WIDTH = 512
D_OUT = 2048
HALF = 256


def tables():
    total = BLOCKS * LEN
    k = np.arange(BLOCKS)
    b = np.arange(LEN)
    first = np.exp(-2j * np.pi * np.outer(k + 0.25, k) / BLOCKS)
    twist = np.exp(-2j * np.pi * np.outer(k + 0.25, b) / total)
    second = np.exp(-2j * np.pi * np.outer(b, b) / LEN)
    eye = np.eye(CH)
    fwd1 = np.kron(np.concatenate([first.real, first.imag]), eye)
    scale = 1.0 / (total * math.sqrt(total))
    inv1 = np.kron(np.concatenate([first.real.T, first.imag.T], 1), eye) * scale
    fwd2 = np.block([[second.real, second.imag], [-second.imag, second.real]])
    inv2 = np.block([[second.real, -second.imag], [second.imag, second.real]])
    cast = lambda a, t: jnp.asarray(np.asarray(a, np.float32)).astype(t)
    rep = lambda a: np.repeat(a, CH, 0)
    return (
        cast(fwd1, bf16),
        cast(fwd2, bf16),
        cast(inv2, bf16),
        cast(inv1, bf16),
        cast(rep(twist.real), f32),
        cast(rep(twist.imag), f32),
        cast(np.eye(HALF), bf16),
    )


def dot(a, b):
    return jnp.dot(a, b, preferred_element_type=f32)


def dot_nt(a, b):
    return lax.dot_general(a, b, (((1,), (1,)), ((), ())), preferred_element_type=f32)


def partner(me, i):
    z, y, x = me // 8, (me // 2) % 4, me % 2
    m, r = i % 8, i // 8
    n = r // 2
    dz = 4 + ((m + 1) // 2) * (1 - 2 * (m % 2))
    dy = 2 + ((n + 1) // 2) * (1 - 2 * (n % 2))
    return ((z + dz) % 8) * 8 + ((y + dy) % 4) * 2 + (x + 1 - r % 2) % 2


def kernel(
    key_h, val_h, qry_h, gout_h, filt_h, wk_h, wq_h, wv_h,
    fwd1_h, fwd2_h, inv2_h, inv1_h, twr_h, twi_h, eye_h,
    gin_ref, gfil_ref,
    key, val, qry, gout, filt, wk, wq, wv,
    fwd1, fwd2, inv2, inv1, twr, twi, eye,
    key_t, val_t, gout_t,
    send, recv, xbuf, spec, ubuf, gbuf, acc,
    sib_out, sib_in, far_out, far_in,
    in_sem, send_sem, recv_sem, rs_send, rs_recv,
):
    me = lax.axis_index("ctx")
    tp = lax.axis_index("tp")
    core = tp % 2
    sib = tp + 1 - 2 * core
    far = (tp + 2) % 4
    diag = 3 - tp

    pairs = [
        (filt_h, filt), (eye_h, eye), (qry_h, qry), (gout_h, gout), (key_h, key), (val_h, val),
        (fwd1_h, fwd1), (twr_h, twr), (twi_h, twi), (fwd2_h, fwd2), (inv2_h, inv2), (inv1_h, inv1),
        (wk_h, wk), (wv_h, wv), (wq_h, wq),
    ]
    loads = [pltpu.make_async_copy(s, d, in_sem.at[n]) for n, (s, d) in enumerate(pairs)]
    for load in loads:
        load.start()

    barrier = pltpu.get_barrier_semaphore()
    for t in (sib, far):
        pl.semaphore_signal(barrier, inc=1, device_id={"tp": t})

    @pl.loop(0, BLOCKS - 1)
    def _(i):
        pl.semaphore_signal(barrier, inc=1, device_id={"ctx": partner(me, i)})

    def flip(src, h):
        return dot_nt(eye[...], src[:, pl.ds(h * HALF, HALF)])

    def post(n):
        pltpu.make_async_copy(send.at[n, me], recv.at[n, me], recv_sem.at[n]).start()

        @pl.loop(0, BLOCKS - 1)
        def _(i):
            d = partner(me, i)
            pltpu.make_async_remote_copy(
                send.at[n, d], recv.at[n, me], send_sem.at[n], recv_sem.at[n],
                device_id={"ctx": d},
            ).start()

    def arrived(n):
        pltpu.make_async_copy(recv.at[n], recv.at[n], recv_sem.at[n]).wait()

    def put_send(n, h, values):
        send[n, pl.ds(h * 32, 32)] = values.reshape(32, CH, LEN).astype(bf16)

    def get_recv(n):
        return recv[n].astype(f32).reshape(ROWS, LEN)

    loads[0].wait()
    loads[1].wait()
    for h in range(2):
        put_send(0, h, flip(filt, h))
    pl.semaphore_wait(barrier, BLOCKS + 1)
    post(0)

    loads[2].wait()
    loads[3].wait()
    for h in range(2):
        rows = pl.ds(h * HALF, HALF)
        g = flip(gout, h)
        gout_t[rows, :] = g.astype(bf16)
        put_send(1, h, flip(qry, h) * g)
    post(1)

    loads[4].wait()
    loads[5].wait()
    for h in range(2):
        rows = pl.ds(h * HALF, HALF)
        a = flip(key, h)
        b = flip(val, h)
        key_t[rows, :] = a.astype(bf16)
        val_t[rows, :] = b.astype(bf16)
        put_send(2, h, a * b)
    post(2)

    def forward(n):
        xbuf[...] = get_recv(n).astype(bf16)

        @pl.loop(0, 2)
        def _(i):
            m = pl.multiple_of(i * HALF, HALF)
            rows = pl.ds(m, HALF)
            yr = dot(fwd1[rows, :], xbuf[...])
            yi = dot(fwd1[pl.ds(m + ROWS, HALF), :], xbuf[...])
            c, s = twr[rows, :], twi[rows, :]
            t = jnp.concatenate([yr * c - yi * s, yr * s + yi * c], axis=1).astype(bf16)
            spec[n, rows, :] = dot(t, fwd2[...])

    def inverse(na, nb, conj, out):
        @pl.loop(0, 2)
        def _(i):
            m = pl.multiple_of(i * HALF, HALF)
            rows = pl.ds(m, HALF)
            ar, ai = spec[na, rows, :LEN], spec[na, rows, LEN:]
            br, bi = spec[nb, rows, :LEN], spec[nb, rows, LEN:]
            if conj:
                yr, yi = ar * br + ai * bi, ai * br - ar * bi
            else:
                yr, yi = ar * br - ai * bi, ar * bi + ai * br
            t = dot(jnp.concatenate([yr, yi], axis=1).astype(bf16), inv2[...])
            tr, ti = t[:, :LEN], t[:, LEN:]
            c, s = twr[rows, :], twi[rows, :]
            ubuf[rows, :] = (tr * c + ti * s).astype(bf16)
            ubuf[pl.ds(m + ROWS, HALF), :] = (ti * c - tr * s).astype(bf16)

        @pl.loop(0, 2)
        def _(i):
            m = pl.multiple_of(i * HALF, HALF)
            y = dot(inv1[pl.ds(m, HALF), :], ubuf[...])
            send[out, pl.ds(i * 32, 32)] = y.reshape(32, CH, LEN).astype(bf16)

    for load in loads[6:12]:
        load.wait()
    arrived(0)
    forward(0)
    arrived(1)
    forward(1)
    inverse(1, 0, True, 3)
    post(3)
    arrived(2)
    forward(2)
    inverse(2, 0, False, 4)
    post(4)
    inverse(1, 2, True, 5)
    post(5)

    for load in loads[12:]:
        load.wait()
    arrived(3)
    back = get_recv(3)
    gbuf[0] = (back * val_t[...].astype(f32)).astype(bf16)
    gbuf[1] = (back * key_t[...].astype(f32)).astype(bf16)

    @pl.loop(0, D_OUT // HALF)
    def _(i):
        rows = pl.ds(pl.multiple_of(i * HALF, HALF), HALF)
        acc[rows, :] = dot(wk[rows, :], gbuf[0]) + dot(wv[rows, :], gbuf[1])

    def to_sib(n, h):
        return pltpu.make_async_remote_copy(
            sib_out.at[n, h], sib_in.at[n, h], rs_send.at[n, h], rs_recv.at[n, h],
            device_id={"tp": sib},
        )

    def to_far(h):
        return pltpu.make_async_remote_copy(
            far_out.at[h], far_in.at[h], rs_send.at[2, h], rs_recv.at[2, h], device_id={"tp": far}
        )

    def rows_of(t, h):
        return pl.ds(pl.multiple_of(t * WIDTH + h * HALF, HALF), HALF)

    def term(t, h):
        rows = rows_of(t, h)
        return acc[rows, :] + dot(wq[rows, :], gbuf[2])

    arrived(4)
    gbuf[2] = (get_recv(4) * gout_t[...].astype(f32)).astype(bf16)
    for h in range(2):
        sib_out[0, h] = term(diag, h).astype(bf16)
        to_sib(0, h).start()
    for h in range(2):
        mine = term(far, h)
        to_sib(0, h).wait_recv()
        far_out[h] = (mine + sib_in[0, h].astype(f32)).astype(bf16)
        to_far(h).start()
    for h in range(2):
        sib_out[1, h] = term(sib, h).astype(bf16)
        to_sib(1, h).start()
    for h in range(2):
        acc[rows_of(tp, h), :] = term(tp, h)
    for h in range(2):
        to_sib(1, h).wait_recv()
        acc[rows_of(tp, h), :] += sib_in[1, h].astype(f32)
    arrived(5)
    gfil_ref[...] = get_recv(5).astype(bf16)
    for h in range(2):
        to_far(h).wait_recv()
        gin_ref[pl.ds(h * HALF, HALF), :] = (acc[rows_of(tp, h), :] + far_in[h].astype(f32)).astype(bf16)

    for n in range(6):
        some = send.at[n, pl.ds(0, BLOCKS - 1)]
        pltpu.make_async_copy(some, some, send_sem.at[n]).wait()
    for h in range(2):
        to_sib(0, h).wait_send()
        to_sib(1, h).wait_send()
        to_far(h).wait_send()


def turn(gin_t, gfil_t, gin_ref, gfil_ref):
    row = lax.broadcasted_iota(jnp.int32, (LEN, LEN), 0)
    col = lax.broadcasted_iota(jnp.int32, (LEN, LEN), 1)
    eye = jnp.where(row == col, 1.0, 0.0).astype(bf16)
    gin_ref[...] = dot_nt(eye, gin_t[...]).astype(bf16)
    gfil_ref[...] = dot_nt(eye, gfil_t[...]).astype(bf16)


def per_device(key_act, value_act, query_act, grad_out, long_filter, w_key, w_query, w_value):
    consts = tables()
    act = lambda: pltpu.VMEM((LEN, WIDTH), bf16)
    weight = lambda: pltpu.VMEM((D_OUT, WIDTH), bf16)
    turned = lambda: pltpu.VMEM((WIDTH, LEN), bf16)
    dma = pltpu.SemaphoreType.DMA
    gin_t, gfil_t = pl.pallas_call(
        kernel,
        out_shape=(jax.ShapeDtypeStruct((WIDTH, LEN), bf16),) * 2,
        in_specs=[pl.BlockSpec(memory_space=pl.ANY)] * 15,
        out_specs=[pl.BlockSpec(memory_space=pltpu.VMEM)] * 2,
        scratch_shapes=[act()] * 5
        + [weight()] * 3
        + [pltpu.VMEM(c.shape, c.dtype) for c in consts]
        + [turned()] * 3
        + [
            pltpu.VMEM((6, BLOCKS, CH, LEN), bf16),
            pltpu.VMEM((6, BLOCKS, CH, LEN), bf16),
            pltpu.VMEM((ROWS, LEN), bf16),
            pltpu.VMEM((3, ROWS, 2 * LEN), f32),
            pltpu.VMEM((2 * ROWS, LEN), bf16),
            pltpu.VMEM((3, WIDTH, LEN), bf16),
            pltpu.VMEM((D_OUT, LEN), f32),
            pltpu.VMEM((2, 2, HALF, LEN), bf16),
            pltpu.VMEM((2, 2, HALF, LEN), bf16),
            pltpu.VMEM((2, HALF, LEN), bf16),
            pltpu.VMEM((2, HALF, LEN), bf16),
            dma((15,)),
            dma((6,)),
            dma((6,)),
            dma((3, 2)),
            dma((3, 2)),
        ],
        compiler_params=pltpu.CompilerParams(
            collective_id=1, has_side_effects=True, vmem_limit_bytes=56 * 2**20
        ),
    )(key_act, value_act, query_act, grad_out, long_filter, w_key, w_query, w_value, *consts)
    return pl.pallas_call(
        turn,
        out_shape=(jax.ShapeDtypeStruct((LEN, WIDTH), bf16),) * 2,
        in_specs=[pl.BlockSpec(memory_space=pltpu.VMEM)] * 2,
        out_specs=[pl.BlockSpec(memory_space=pltpu.VMEM)] * 2,
    )(gin_t, gfil_t)


def solution(mesh):
    placed = (P("ctx", "tp"),) * 5 + (P(None, "tp"),) * 3
    return jax.shard_map(
        per_device,
        mesh=mesh,
        in_specs=placed,
        out_specs=(P("ctx", "tp"), P("ctx", "tp")),
        check_vma=False,
    )
```

```python
import functools
import math

import jax
import jax.numpy as jnp
import numpy as np
from jax import lax
from jax.experimental import pallas as pl
from jax.experimental.pallas import tpu as pltpu
from jax.sharding import PartitionSpec as P

f32 = jnp.float32
bf16 = jnp.bfloat16
BLOCKS = 64
CH = 8
LEN = 256
ROWS = BLOCKS * CH
WIDTH = 512
D_OUT = 2048
HALF = 256
PIECES = 8
PIECE = WIDTH // PIECES


def tables():
    total = BLOCKS * LEN
    k = np.arange(BLOCKS)
    b = np.arange(LEN)
    first = np.exp(-2j * np.pi * np.outer(k + 0.25, k) / BLOCKS)
    twist = np.exp(-2j * np.pi * np.outer(k + 0.25, b) / total)
    second = np.exp(-2j * np.pi * np.outer(b, b) / LEN)
    eye = np.eye(CH)
    fwd1 = np.kron(np.concatenate([first.real, first.imag]), eye)
    scale = 1.0 / (total * math.sqrt(total))
    inv1 = np.kron(np.concatenate([first.real.T, first.imag.T], 1), eye) * scale
    fwd2 = np.block([[second.real, second.imag], [-second.imag, second.real]])
    inv2 = np.block([[second.real, -second.imag], [second.imag, second.real]])
    cast = lambda a, t: jnp.asarray(np.asarray(a, np.float32)).astype(t)
    rep = lambda a: np.repeat(a, CH, 0)
    return (
        cast(fwd1, bf16),
        cast(fwd2, bf16),
        cast(inv2, bf16),
        cast(inv1, bf16),
        cast(rep(twist.real), f32),
        cast(rep(twist.imag), f32),
        cast(np.eye(HALF), bf16),
    )


def dot(a, b):
    return jnp.dot(a, b, preferred_element_type=f32)


def dot_nt(a, b):
    return lax.dot_general(a, b, (((1,), (1,)), ((), ())), preferred_element_type=f32)


def partner(me, i):
    z, y, x = me // 8, (me // 2) % 4, me % 2
    m, r = i % 8, i // 8
    n = r // 2
    dz = 4 + ((m + 1) // 2) * (1 - 2 * (m % 2))
    dy = 2 + ((n + 1) // 2) * (1 - 2 * (n % 2))
    return ((z + dz) % 8) * 8 + ((y + dy) % 4) * 2 + (x + 1 - r % 2) % 2


def kernel(
    key_h, val_h, qry_h, gout_h, filt_h, wk_h, wq_h, wv_h,
    fwd1_h, fwd2_h, inv2_h, inv1_h, twr_h, twi_h, eye_h,
    gin_ref, gfil_ref,
    key, val, qry, gout, filt, wk, wq, wv,
    fwd1, fwd2, inv2, inv1, twr, twi, eye,
    key_t, val_t, gout_t,
    send, recv, xbuf, spec, ubuf, gbuf, acc,
    sib_out, sib_in, far_out, far_in,
    in_sem, send_sem, recv_sem, rs_send, rs_recv,
):
    me = lax.axis_index("ctx")
    tp = lax.axis_index("tp")
    core = tp % 2
    sib = tp + 1 - 2 * core
    far = (tp + 2) % 4
    diag = 3 - tp

    barrier = pltpu.get_barrier_semaphore()
    for t in (sib, far):
        pl.semaphore_signal(barrier, inc=1, device_id={"tp": t})

    @pl.loop(0, BLOCKS - 1)
    def _(i):
        pl.semaphore_signal(barrier, inc=1, device_id={"ctx": partner(me, i)})

    pairs = [
        (filt_h, filt), (eye_h, eye), (qry_h, qry), (gout_h, gout), (key_h, key), (val_h, val),
        (fwd1_h, fwd1), (twr_h, twr), (twi_h, twi), (fwd2_h, fwd2), (inv2_h, inv2), (inv1_h, inv1),
        (wk_h, wk), (wv_h, wv), (wq_h, wq),
    ]
    loads = [pltpu.make_async_copy(s, d, in_sem.at[n]) for n, (s, d) in enumerate(pairs)]
    for load in loads:
        load.start()

    def flip(src, h):
        return dot_nt(eye[...], src[:, pl.ds(h * HALF, HALF)])

    def post(n):
        pltpu.make_async_copy(send.at[n, me], recv.at[n, me], recv_sem.at[n]).start()

        @pl.loop(0, BLOCKS - 1)
        def _(i):
            d = partner(me, i)
            pltpu.make_async_remote_copy(
                send.at[n, d], recv.at[n, me], send_sem.at[n], recv_sem.at[n],
                device_id={"ctx": d},
            ).start()

    def arrived(n):
        pltpu.make_async_copy(recv.at[n], recv.at[n], recv_sem.at[n]).wait()

    def put_send(n, h, values):
        send[n, pl.ds(h * 32, 32)] = values.reshape(32, CH, LEN).astype(bf16)

    def get_recv(n):
        return recv[n].astype(f32).reshape(ROWS, LEN)

    loads[0].wait()
    loads[1].wait()
    for h in range(2):
        put_send(0, h, flip(filt, h))
    pl.semaphore_wait(barrier, BLOCKS + 1)
    post(0)

    loads[2].wait()
    loads[3].wait()
    for h in range(2):
        rows = pl.ds(h * HALF, HALF)
        g = flip(gout, h)
        gout_t[rows, :] = g.astype(bf16)
        put_send(1, h, flip(qry, h) * g)
    post(1)

    loads[4].wait()
    loads[5].wait()
    for h in range(2):
        rows = pl.ds(h * HALF, HALF)
        a = flip(key, h)
        b = flip(val, h)
        key_t[rows, :] = a.astype(bf16)
        val_t[rows, :] = b.astype(bf16)
        put_send(2, h, a * b)
    post(2)

    def forward(n):
        xbuf[...] = get_recv(n).astype(bf16)

        @pl.loop(0, 2, unroll=True)
        def _(i):
            m = pl.multiple_of(i * HALF, HALF)
            rows = pl.ds(m, HALF)
            yr = dot(fwd1[rows, :], xbuf[...])
            yi = dot(fwd1[pl.ds(m + ROWS, HALF), :], xbuf[...])
            c, s = twr[rows, :], twi[rows, :]
            t = jnp.concatenate([yr * c - yi * s, yr * s + yi * c], axis=1).astype(bf16)
            spec[n, rows, :] = dot(t, fwd2[...])

    def inverse(na, nb, conj, out):
        @pl.loop(0, 2, unroll=True)
        def _(i):
            m = pl.multiple_of(i * HALF, HALF)
            rows = pl.ds(m, HALF)
            ar, ai = spec[na, rows, :LEN], spec[na, rows, LEN:]
            br, bi = spec[nb, rows, :LEN], spec[nb, rows, LEN:]
            if conj:
                yr, yi = ar * br + ai * bi, ai * br - ar * bi
            else:
                yr, yi = ar * br - ai * bi, ar * bi + ai * br
            t = dot(jnp.concatenate([yr, yi], axis=1).astype(bf16), inv2[...])
            tr, ti = t[:, :LEN], t[:, LEN:]
            c, s = twr[rows, :], twi[rows, :]
            ubuf[rows, :] = (tr * c + ti * s).astype(bf16)
            ubuf[pl.ds(m + ROWS, HALF), :] = (ti * c - tr * s).astype(bf16)

        @pl.loop(0, 2, unroll=True)
        def _(i):
            m = pl.multiple_of(i * HALF, HALF)
            y = dot(inv1[pl.ds(m, HALF), :], ubuf[...])
            send[out, pl.ds(i * 32, 32)] = y.reshape(32, CH, LEN).astype(bf16)

    for load in loads[6:12]:
        load.wait()
    arrived(0)
    forward(0)
    arrived(1)
    forward(1)
    inverse(1, 0, True, 3)
    post(3)
    arrived(2)
    forward(2)
    inverse(2, 0, False, 4)
    post(4)
    inverse(1, 2, True, 5)
    post(5)

    for load in loads[12:]:
        load.wait()
    arrived(3)
    back = get_recv(3)
    gbuf[0] = (back * val_t[...].astype(f32)).astype(bf16)
    gbuf[1] = (back * key_t[...].astype(f32)).astype(bf16)

    @pl.loop(0, D_OUT // HALF)
    def _(i):
        rows = pl.ds(pl.multiple_of(i * HALF, HALF), HALF)
        acc[rows, :] = dot(wk[rows, :], gbuf[0]) + dot(wv[rows, :], gbuf[1])

    def to_sib(n, h):
        return pltpu.make_async_remote_copy(
            sib_out.at[n, h], sib_in.at[n, h], rs_send.at[n, h], rs_recv.at[n, h],
            device_id={"tp": sib},
        )

    def to_far(h):
        return pltpu.make_async_remote_copy(
            far_out.at[h], far_in.at[h], rs_send.at[2, h], rs_recv.at[2, h], device_id={"tp": far}
        )

    def rows_of(t, h):
        return pl.ds(pl.multiple_of(t * WIDTH + h * PIECE, PIECE), PIECE)

    def term(t, h):
        rows = rows_of(t, h)
        return acc[rows, :] + dot(wq[rows, :], gbuf[2])

    arrived(4)
    gbuf[2] = (get_recv(4) * gout_t[...].astype(f32)).astype(bf16)
    for h in range(PIECES):
        sib_out[0, h] = term(diag, h).astype(bf16)
        to_sib(0, h).start()
    for h in range(PIECES):
        mine = term(far, h)
        to_sib(0, h).wait_recv()
        far_out[h] = (mine + sib_in[0, h].astype(f32)).astype(bf16)
        to_far(h).start()
    for h in range(PIECES):
        sib_out[1, h] = term(sib, h).astype(bf16)
        to_sib(1, h).start()
    for h in range(PIECES):
        acc[rows_of(tp, h), :] = term(tp, h)
    for h in range(PIECES):
        to_sib(1, h).wait_recv()
        acc[rows_of(tp, h), :] += sib_in[1, h].astype(f32)
    arrived(5)
    gfil_ref[...] = get_recv(5).astype(bf16)
    for h in range(PIECES):
        to_far(h).wait_recv()
        gin_ref[pl.ds(h * PIECE, PIECE), :] = (acc[rows_of(tp, h), :] + far_in[h].astype(f32)).astype(bf16)

    for n in range(6):
        some = send.at[n, pl.ds(0, BLOCKS - 1)]
        pltpu.make_async_copy(some, some, send_sem.at[n]).wait()
    for h in range(PIECES):
        to_sib(0, h).wait_send()
        to_sib(1, h).wait_send()
        to_far(h).wait_send()


def turn(gin_t, gfil_t, gin_ref, gfil_ref):
    row = lax.broadcasted_iota(jnp.int32, (LEN, LEN), 0)
    col = lax.broadcasted_iota(jnp.int32, (LEN, LEN), 1)
    eye = jnp.where(row == col, 1.0, 0.0).astype(bf16)
    gin_ref[...] = dot_nt(eye, gin_t[...]).astype(bf16)
    gfil_ref[...] = dot_nt(eye, gfil_t[...]).astype(bf16)


def per_device(key_act, value_act, query_act, grad_out, long_filter, w_key, w_query, w_value):
    consts = tables()
    act = lambda: pltpu.VMEM((LEN, WIDTH), bf16)
    weight = lambda: pltpu.VMEM((D_OUT, WIDTH), bf16)
    turned = lambda: pltpu.VMEM((WIDTH, LEN), bf16)
    dma = pltpu.SemaphoreType.DMA
    gin_t, gfil_t = pl.pallas_call(
        kernel,
        out_shape=(jax.ShapeDtypeStruct((WIDTH, LEN), bf16),) * 2,
        in_specs=[pl.BlockSpec(memory_space=pl.ANY)] * 15,
        out_specs=[pl.BlockSpec(memory_space=pltpu.VMEM)] * 2,
        scratch_shapes=[act()] * 5
        + [weight()] * 3
        + [pltpu.VMEM(c.shape, c.dtype) for c in consts]
        + [turned()] * 3
        + [
            pltpu.VMEM((6, BLOCKS, CH, LEN), bf16),
            pltpu.VMEM((6, BLOCKS, CH, LEN), bf16),
            pltpu.VMEM((ROWS, LEN), bf16),
            pltpu.VMEM((3, ROWS, 2 * LEN), f32),
            pltpu.VMEM((2 * ROWS, LEN), bf16),
            pltpu.VMEM((3, WIDTH, LEN), bf16),
            pltpu.VMEM((D_OUT, LEN), f32),
            pltpu.VMEM((2, PIECES, PIECE, LEN), bf16),
            pltpu.VMEM((2, PIECES, PIECE, LEN), bf16),
            pltpu.VMEM((PIECES, PIECE, LEN), bf16),
            pltpu.VMEM((PIECES, PIECE, LEN), bf16),
            dma((15,)),
            dma((6,)),
            dma((6,)),
            dma((3, PIECES)),
            dma((3, PIECES)),
        ],
        compiler_params=pltpu.CompilerParams(
            collective_id=1, has_side_effects=True, vmem_limit_bytes=56 * 2**20
        ),
    )(key_act, value_act, query_act, grad_out, long_filter, w_key, w_query, w_value, *consts)
    return pl.pallas_call(
        turn,
        out_shape=(jax.ShapeDtypeStruct((LEN, WIDTH), bf16),) * 2,
        in_specs=[pl.BlockSpec(memory_space=pltpu.VMEM)] * 2,
        out_specs=[pl.BlockSpec(memory_space=pltpu.VMEM)] * 2,
    )(gin_t, gfil_t)


def solution(mesh):
    placed = (P("ctx", "tp"),) * 5 + (P(None, "tp"),) * 3
    return jax.shard_map(
        per_device,
        mesh=mesh,
        in_specs=placed,
        out_specs=(P("ctx", "tp"), P("ctx", "tp")),
        check_vma=False,
    )
```

```python
import functools
import math

import jax
import jax.numpy as jnp
import numpy as np
from jax import lax
from jax.experimental import pallas as pl
from jax.experimental.pallas import tpu as pltpu
from jax.sharding import PartitionSpec as P

f32 = jnp.float32
bf16 = jnp.bfloat16
BLOCKS = 64
CH = 8
LEN = 256
ROWS = BLOCKS * CH
WIDTH = 512
D_OUT = 2048
HALF = 256
PIECES = 8
PIECE = WIDTH // PIECES


def tables():
    total = BLOCKS * LEN
    k = np.arange(BLOCKS)
    b = np.arange(LEN)
    first = np.exp(-2j * np.pi * np.outer(k + 0.25, k) / BLOCKS)
    twist = np.exp(-2j * np.pi * np.outer(k + 0.25, b) / total)
    second = np.exp(-2j * np.pi * np.outer(b, b) / LEN)
    eye = np.eye(CH)
    fwd1 = np.kron(np.concatenate([first.real, first.imag]), eye)
    scale = 1.0 / (total * math.sqrt(total))
    inv1 = np.kron(np.concatenate([first.real.T, first.imag.T], 1), eye) * scale
    fwd2 = np.block([[second.real, second.imag], [-second.imag, second.real]])
    inv2 = np.block([[second.real, -second.imag], [second.imag, second.real]])
    cast = lambda a, t: jnp.asarray(np.asarray(a, np.float32)).astype(t)
    rep = lambda a: np.repeat(a, CH, 0)
    return (
        cast(fwd1, bf16),
        cast(fwd2, bf16),
        cast(inv2, bf16),
        cast(inv1, bf16),
        cast(rep(twist.real), f32),
        cast(rep(twist.imag), f32),
        cast(np.eye(HALF), bf16),
    )


def dot(a, b):
    return jnp.dot(a, b, preferred_element_type=f32)


def dot_nt(a, b):
    return lax.dot_general(a, b, (((1,), (1,)), ((), ())), preferred_element_type=f32)


def partner(me, i):
    z, y, x = me // 8, (me // 2) % 4, me % 2
    m, r = i % 8, i // 8
    n = r // 2
    dz = 4 + ((m + 1) // 2) * (1 - 2 * (m % 2))
    dy = 2 + ((n + 1) // 2) * (1 - 2 * (n % 2))
    return ((z + dz) % 8) * 8 + ((y + dy) % 4) * 2 + (x + 1 - r % 2) % 2


def kernel(
    key_h, val_h, qry_h, gout_h, filt_h, wk_h, wq_h, wv_h,
    fwd1_h, fwd2_h, inv2_h, inv1_h, twr_h, twi_h, eye_h,
    gin_h, gfil_h,
    key, val, qry, gout, filt, wk, wq, wv,
    fwd1, fwd2, inv2, inv1, twr, twi, eye,
    key_t, val_t, gout_t,
    send, recv, xbuf, spec, ubuf, gbuf, acc,
    sib_out, sib_in, far_out, far_in,
    gin_ref, gfil_ref, in_sem, send_sem, recv_sem, rs_send, rs_recv, out_sem,
):
    me = lax.axis_index("ctx")
    tp = lax.axis_index("tp")
    core = tp % 2
    sib = tp + 1 - 2 * core
    far = (tp + 2) % 4
    diag = 3 - tp

    barrier = pltpu.get_barrier_semaphore()
    for t in (sib, far):
        pl.semaphore_signal(barrier, inc=1, device_id={"tp": t})

    @pl.loop(0, BLOCKS - 1)
    def _(i):
        pl.semaphore_signal(barrier, inc=1, device_id={"ctx": partner(me, i)})

    pairs = [
        (filt_h, filt), (eye_h, eye), (qry_h, qry), (gout_h, gout), (key_h, key), (val_h, val),
        (fwd1_h, fwd1), (twr_h, twr), (twi_h, twi), (fwd2_h, fwd2), (inv2_h, inv2), (inv1_h, inv1),
        (wk_h, wk), (wv_h, wv), (wq_h, wq),
    ]
    loads = [pltpu.make_async_copy(s, d, in_sem.at[n]) for n, (s, d) in enumerate(pairs)]
    for load in loads:
        load.start()

    def flip(src, h):
        return dot_nt(eye[...], src[:, pl.ds(h * HALF, HALF)])

    def post(n):
        pltpu.make_async_copy(send.at[n, me], recv.at[n, me], recv_sem.at[n]).start()

        @pl.loop(0, BLOCKS - 1)
        def _(i):
            d = partner(me, i)
            pltpu.make_async_remote_copy(
                send.at[n, d], recv.at[n, me], send_sem.at[n], recv_sem.at[n],
                device_id={"ctx": d},
            ).start()

    def arrived(n):
        pltpu.make_async_copy(recv.at[n], recv.at[n], recv_sem.at[n]).wait()

    def put_send(n, h, values):
        send[n, pl.ds(h * 32, 32)] = values.reshape(32, CH, LEN).astype(bf16)

    def get_recv(n):
        return recv[n].astype(f32).reshape(ROWS, LEN)

    loads[0].wait()
    loads[1].wait()
    for h in range(2):
        put_send(0, h, flip(filt, h))
    pl.semaphore_wait(barrier, BLOCKS + 1)
    post(0)

    loads[2].wait()
    loads[3].wait()
    for h in range(2):
        rows = pl.ds(h * HALF, HALF)
        g = flip(gout, h)
        gout_t[rows, :] = g.astype(bf16)
        put_send(1, h, flip(qry, h) * g)
    post(1)

    loads[4].wait()
    loads[5].wait()
    for h in range(2):
        rows = pl.ds(h * HALF, HALF)
        a = flip(key, h)
        b = flip(val, h)
        key_t[rows, :] = a.astype(bf16)
        val_t[rows, :] = b.astype(bf16)
        put_send(2, h, a * b)
    post(2)

    def forward(n):
        xbuf[...] = get_recv(n).astype(bf16)

        @pl.loop(0, 2, unroll=True)
        def _(i):
            m = pl.multiple_of(i * HALF, HALF)
            rows = pl.ds(m, HALF)
            yr = dot(fwd1[rows, :], xbuf[...])
            yi = dot(fwd1[pl.ds(m + ROWS, HALF), :], xbuf[...])
            c, s = twr[rows, :], twi[rows, :]
            t = jnp.concatenate([yr * c - yi * s, yr * s + yi * c], axis=1).astype(bf16)
            spec[n, rows, :] = dot(t, fwd2[...])

    def inverse(na, nb, conj, out):
        @pl.loop(0, 2, unroll=True)
        def _(i):
            m = pl.multiple_of(i * HALF, HALF)
            rows = pl.ds(m, HALF)
            ar, ai = spec[na, rows, :LEN], spec[na, rows, LEN:]
            br, bi = spec[nb, rows, :LEN], spec[nb, rows, LEN:]
            if conj:
                yr, yi = ar * br + ai * bi, ai * br - ar * bi
            else:
                yr, yi = ar * br - ai * bi, ar * bi + ai * br
            t = dot(jnp.concatenate([yr, yi], axis=1).astype(bf16), inv2[...])
            tr, ti = t[:, :LEN], t[:, LEN:]
            c, s = twr[rows, :], twi[rows, :]
            ubuf[rows, :] = (tr * c + ti * s).astype(bf16)
            ubuf[pl.ds(m + ROWS, HALF), :] = (ti * c - tr * s).astype(bf16)

        @pl.loop(0, 2, unroll=True)
        def _(i):
            m = pl.multiple_of(i * HALF, HALF)
            y = dot(inv1[pl.ds(m, HALF), :], ubuf[...])
            send[out, pl.ds(i * 32, 32)] = y.reshape(32, CH, LEN).astype(bf16)

    for load in loads[6:12]:
        load.wait()
    arrived(0)
    forward(0)
    arrived(1)
    forward(1)
    inverse(1, 0, True, 3)
    post(3)
    arrived(2)
    forward(2)
    inverse(2, 0, False, 4)
    post(4)
    inverse(1, 2, True, 5)
    post(5)

    for load in loads[12:]:
        load.wait()
    arrived(3)
    back = get_recv(3)
    gbuf[0] = (back * val_t[...].astype(f32)).astype(bf16)
    gbuf[1] = (back * key_t[...].astype(f32)).astype(bf16)

    @pl.loop(0, D_OUT // HALF, unroll=4)
    def _(i):
        rows = pl.ds(pl.multiple_of(i * HALF, HALF), HALF)
        acc[rows, :] = dot(wk[rows, :], gbuf[0]) + dot(wv[rows, :], gbuf[1])

    def to_sib(n, h):
        return pltpu.make_async_remote_copy(
            sib_out.at[n, h], sib_in.at[n, h], rs_send.at[n, h], rs_recv.at[n, h],
            device_id={"tp": sib},
        )

    def to_far(h):
        return pltpu.make_async_remote_copy(
            far_out.at[h], far_in.at[h], rs_send.at[2, h], rs_recv.at[2, h], device_id={"tp": far}
        )

    def rows_of(t, h):
        return pl.ds(pl.multiple_of(t * WIDTH + h * PIECE, PIECE), PIECE)

    def term(t, h):
        rows = rows_of(t, h)
        return acc[rows, :] + dot(wq[rows, :], gbuf[2])

    arrived(4)
    gbuf[2] = (get_recv(4) * gout_t[...].astype(f32)).astype(bf16)
    for h in range(PIECES):
        sib_out[0, h] = term(diag, h).astype(bf16)
        to_sib(0, h).start()
    for h in range(PIECES):
        mine = term(far, h)
        to_sib(0, h).wait_recv()
        far_out[h] = (mine + sib_in[0, h].astype(f32)).astype(bf16)
        to_far(h).start()
    for h in range(PIECES):
        sib_out[1, h] = term(sib, h).astype(bf16)
        to_sib(1, h).start()
    for h in range(PIECES):
        acc[rows_of(tp, h), :] = term(tp, h)
    for h in range(PIECES):
        to_sib(1, h).wait_recv()
        acc[rows_of(tp, h), :] += sib_in[1, h].astype(f32)
    arrived(5)
    gfil_ref[...] = get_recv(5).astype(bf16)
    outs = [pltpu.make_async_copy(gfil_ref, gfil_h, out_sem.at[PIECES])]
    outs[0].start()
    for h in range(PIECES):
        to_far(h).wait_recv()
        gin_ref[pl.ds(h * PIECE, PIECE), :] = (acc[rows_of(tp, h), :] + far_in[h].astype(f32)).astype(bf16)
        rows = pl.ds(h * PIECE, PIECE)
        outs.append(pltpu.make_async_copy(gin_ref.at[rows], gin_h.at[rows], out_sem.at[h]))
        outs[-1].start()

    for out in outs:
        out.wait()

    for n in range(6):
        some = send.at[n, pl.ds(0, BLOCKS - 1)]
        pltpu.make_async_copy(some, some, send_sem.at[n]).wait()
    for h in range(PIECES):
        to_sib(0, h).wait_send()
        to_sib(1, h).wait_send()
        to_far(h).wait_send()


def turn(gin_t, gfil_t, gin_ref, gfil_ref):
    row = lax.broadcasted_iota(jnp.int32, (LEN, LEN), 0)
    col = lax.broadcasted_iota(jnp.int32, (LEN, LEN), 1)
    eye = jnp.where(row == col, 1.0, 0.0).astype(bf16)
    gin_ref[...] = dot_nt(eye, gin_t[...]).astype(bf16)
    gfil_ref[...] = dot_nt(eye, gfil_t[...]).astype(bf16)


def per_device(key_act, value_act, query_act, grad_out, long_filter, w_key, w_query, w_value):
    consts = tables()
    act = lambda: pltpu.VMEM((LEN, WIDTH), bf16)
    weight = lambda: pltpu.VMEM((D_OUT, WIDTH), bf16)
    turned = lambda: pltpu.VMEM((WIDTH, LEN), bf16)
    dma = pltpu.SemaphoreType.DMA
    gin_t, gfil_t = pl.pallas_call(
        kernel,
        out_shape=(jax.ShapeDtypeStruct((WIDTH, LEN), bf16),) * 2,
        in_specs=[pl.BlockSpec(memory_space=pl.ANY)] * 15,
        out_specs=[pl.BlockSpec(memory_space=pl.ANY)] * 2,
        scratch_shapes=[act()] * 5
        + [weight()] * 3
        + [pltpu.VMEM(c.shape, c.dtype) for c in consts]
        + [turned()] * 3
        + [
            pltpu.VMEM((6, BLOCKS, CH, LEN), bf16),
            pltpu.VMEM((6, BLOCKS, CH, LEN), bf16),
            pltpu.VMEM((ROWS, LEN), bf16),
            pltpu.VMEM((3, ROWS, 2 * LEN), f32),
            pltpu.VMEM((2 * ROWS, LEN), bf16),
            pltpu.VMEM((3, WIDTH, LEN), bf16),
            pltpu.VMEM((D_OUT, LEN), f32),
            pltpu.VMEM((2, PIECES, PIECE, LEN), bf16),
            pltpu.VMEM((2, PIECES, PIECE, LEN), bf16),
            pltpu.VMEM((PIECES, PIECE, LEN), bf16),
            pltpu.VMEM((PIECES, PIECE, LEN), bf16),
            turned(),
            turned(),
            dma((15,)),
            dma((6,)),
            dma((6,)),
            dma((3, PIECES)),
            dma((3, PIECES)),
            dma((PIECES + 1,)),
        ],
        compiler_params=pltpu.CompilerParams(
            collective_id=1, has_side_effects=True, vmem_limit_bytes=56 * 2**20
        ),
    )(key_act, value_act, query_act, grad_out, long_filter, w_key, w_query, w_value, *consts)
    return pl.pallas_call(
        turn,
        out_shape=(jax.ShapeDtypeStruct((LEN, WIDTH), bf16),) * 2,
        in_specs=[pl.BlockSpec(memory_space=pltpu.VMEM)] * 2,
        out_specs=[pl.BlockSpec(memory_space=pltpu.VMEM)] * 2,
    )(gin_t, gfil_t)


def solution(mesh):
    placed = (P("ctx", "tp"),) * 5 + (P(None, "tp"),) * 3
    return jax.shard_map(
        per_device,
        mesh=mesh,
        in_specs=placed,
        out_specs=(P("ctx", "tp"), P("ctx", "tp")),
        check_vma=False,
    )
```
